32 devices in a mesh: slab: 2 (over y), docs: 4 (over x, core), blk: 4 (over z).
Axes of the slice: x: 2, y: 2, z: 4, core: 2. Of those that a mesh axis runs over, the one named last changes fastest.
Arguments:
- pooled: bfloat16 [16384, 768], P(('slab', 'docs', 'blk')), parts along dimension 0, may hold values from -6 to 6
- proj_weight: bfloat16 [768, 768], replicated, may hold values from -0.21875 to 0.21875
- cluster: int32 [16384], P(('slab', 'docs', 'blk')), parts along dimension 0, may hold values from 0 to 143, as said below
Outputs:
- best_sim: float32 [16384], P(('slab', 'docs', 'blk')), parts along dimension 0
The draws below stay inside these ranges and needn't reach their ends.
There are 2 independent parts, one for each index of `slab`. The reference program is written for one: setup_inputs(seed, part) draws one part's arguments, and reference() takes and returns one part's arrays. A program takes and returns all parts, laid end to end along the dimension named above; an argument that names none is the same for every part. Nothing has to cross between parts.
Inputs may be any that keep to these rules, and one draw needn't show every extreme that they name: Clusters below 16 are large, the others small. The documents of one device hold exactly 128 of large clusters and 384 of small ones. Among one device's documents at most 64 of large clusters share the value of cluster modulo the size of docs, and at most 48 of small clusters share the value of (cluster - 16) modulo the number of devices of docs and blk; in every draw one value of each kind holds exactly that many on every device.
All inputs are finite; a program needn't handle non-finite values.
Results may differ from the reference program's by a relative error of at most 0.0012.
Values may be sent and summed in bfloat16 or wider, within the bound.
A program may use at most 64 MiB of HBM per device.

```python
import jax
import jax.numpy as jnp
from jax import lax

D = 768
BIG_OWN = 4
SMALL_OWN = 8
BIG_DEV = 128
SMALL_DEV = 384
LARGE_CL = 16
CAPB = 64
CAPS = 48
DOCS = 8192
N_DOCS = 4
N_BLK = 4


def draw_cluster(key, part):
    devices = N_DOCS * N_BLK
    hot_owner = jax.random.randint(jax.random.fold_in(key, 11), (), 0, N_DOCS).astype(jnp.int32)
    hot_target = jax.random.randint(jax.random.fold_in(key, 12), (), 0, devices).astype(jnp.int32)
    device_keys = jax.random.split(jax.random.fold_in(key, 13), devices)

    def one_device(device_key):
        subkeys = jax.random.split(device_key, 7)
        big_slots = N_DOCS * CAPB
        big_owner = jnp.arange(big_slots, dtype=jnp.int32) // CAPB
        big_pri = jnp.where(big_owner == hot_owner, 0, 1) * big_slots + jax.random.permutation(subkeys[0], big_slots).astype(jnp.int32)
        chosen = jnp.argsort(big_pri)[:BIG_DEV]
        owners = big_owner[chosen]
        big_rank = jnp.minimum(jax.random.randint(subkeys[1], (BIG_DEV,), 0, BIG_OWN), jax.random.randint(subkeys[2], (BIG_DEV,), 0, BIG_OWN))
        big_ids = owners + N_DOCS * big_rank
        small_slots = devices * CAPS
        small_target = jnp.arange(small_slots, dtype=jnp.int32) // CAPS
        small_pri = jnp.where(small_target == hot_target, 0, 1) * small_slots + jax.random.permutation(subkeys[3], small_slots).astype(jnp.int32)
        picked = jnp.argsort(small_pri)[:SMALL_DEV]
        targets = small_target[picked]
        small_rank = jnp.minimum(jax.random.randint(subkeys[4], (SMALL_DEV,), 0, SMALL_OWN), jax.random.randint(subkeys[5], (SMALL_DEV,), 0, SMALL_OWN))
        small_ids = LARGE_CL + targets + devices * small_rank
        all_ids = jnp.concatenate([big_ids, small_ids]).astype(jnp.int32)
        return jax.random.permutation(subkeys[6], all_ids)
    return jax.vmap(one_device)(device_keys).reshape(-1).astype(jnp.int32)


def block_scale(own_key, shape, cuts, smallest, top_value):
    level, own = 1.0, jax.random.fold_in(own_key, 6)
    for axis_at, shards_of in cuts:
        steps = jnp.exp(jax.random.uniform(jax.random.fold_in(own, axis_at), (shards_of,), jnp.float32, smallest / len(cuts), top_value / len(cuts)))
        level = level * jnp.repeat(steps, shape[axis_at] // shards_of).reshape([-1 if axis == axis_at else 1 for axis in range(len(shape))])
    return level


def bell_draw(stream_key, shape, width, reach, shards=(), held_as=jnp.bfloat16):
    drawn = jax.random.normal(stream_key, shape, jnp.float32) * width
    if len(shards) > 0:
        drawn = block_scale(stream_key, shape, shards, -0.22, 0.18) * drawn
    return jnp.clip(drawn, min=-reach, max=reach).astype(held_as)


def setup_inputs(seed: int = 0, part: int = 0) -> dict:
    arg_keys = jax.random.split(jax.random.key(seed), 4)
    part_splits = jax.random.split(jax.random.fold_in(arg_keys[3], part), 4)
    return {
        "pooled": bell_draw(part_splits[0], (DOCS, D), 1.0, 6.0, ((0, 16),)),
        "proj_weight": bell_draw(arg_keys[1], (D, D), D ** -0.5, 0.21875),
        "cluster": draw_cluster(jax.random.fold_in(jax.random.fold_in(arg_keys[3], part), 71), part),
    }


def group_best(embedded, cluster, group_of, groups, capacity):
    total_rows = embedded.shape[0]
    feature = embedded.shape[1]
    positions = jnp.arange(total_rows, dtype=jnp.int32)
    group_key = jnp.where(group_of >= 0, group_of, groups).astype(jnp.int32)
    sort_order = jnp.argsort(group_key * total_rows + positions).astype(jnp.int32)
    sorted_key = group_key[sort_order]
    group_sizes = jax.ops.segment_sum(jnp.ones((total_rows,), jnp.int32), group_key, num_segments=groups + 1)
    starts = (jnp.cumsum(group_sizes) - group_sizes).astype(jnp.int32)
    sorted_rank = positions - starts[sorted_key]
    slot_rank = jnp.zeros((total_rows,), jnp.int32).at[sort_order].set(sorted_rank)
    slot = jnp.where(group_of >= 0, group_key * capacity + slot_rank, groups * capacity).astype(jnp.int32)
    padded = jnp.zeros((groups * capacity, feature), embedded.dtype).at[slot].set(embedded, mode='drop')
    padded_ids = jnp.full((groups * capacity,), -1, jnp.int32).at[slot].set(cluster, mode='drop')
    padded = padded.reshape(groups, capacity, feature)
    padded_ids = padded_ids.reshape(groups, capacity)

    def group_scan(operands):
        block_rows, block_ids = operands
        scores = jnp.dot(block_rows, block_rows.T, preferred_element_type=jnp.float32)
        inside = jnp.arange(capacity, dtype=jnp.int32)
        allowed = (block_ids[:, None] == block_ids[None, :]) & (block_ids[:, None] >= 0) & (inside[:, None] != inside[None, :])
        return lax.optimization_barrier(jnp.max(jnp.where(allowed, scores, -1.0), axis=1))
    best_all = lax.map(group_scan, (padded, padded_ids)).reshape(-1)
    return best_all[jnp.minimum(slot, groups * capacity - 1)]

def reference(pooled, proj_weight, cluster):
    projected = jnp.dot(pooled, proj_weight, preferred_element_type=jnp.float32)
    embedded = (projected / jnp.sqrt(lax.optimization_barrier(jnp.sum(projected * projected, axis=1, keepdims=True)) + 1e-06)).astype(jnp.bfloat16)
    is_big = cluster < LARGE_CL
    big_group = jnp.where(is_big, cluster % N_DOCS, -1).astype(jnp.int32)
    small_group = jnp.where(is_big, -1, (cluster - LARGE_CL) % (N_DOCS * N_BLK)).astype(jnp.int32)
    best_big = group_best(embedded, cluster, big_group, N_DOCS, N_DOCS * N_BLK * CAPB)
    best_small = group_best(embedded, cluster, small_group, N_DOCS * N_BLK, N_DOCS * N_BLK * CAPS)
    return jnp.where(is_big, best_big, best_small)
```

```python
import functools

import jax
import jax.numpy as jnp
from jax import lax
from jax.experimental import pallas as pl
from jax.experimental.pallas import tpu as pltpu
from jax.sharding import PartitionSpec as P

MESH = pl.DeviceIdType.MESH
BIG_OWN = 4
LANES = 128
F32 = jnp.float32
BF16 = jnp.bfloat16


def up(value, step):
    return -(-value // step) * step


def iota(shape, dim):
    return lax.broadcasted_iota(jnp.int32, shape, dim)


def nt(a, b):
    return lax.dot_general(a, b, (((1,), (1,)), ((), ())), preferred_element_type=F32)


def exact_dot(a, b):
    return jnp.dot(a, b, preferred_element_type=F32, precision=lax.Precision.HIGHEST)


def kernel(
    dims, pooled_hbm, weight_hbm, cluster_ref, out_ref,
    pooled, weight, embedded, small_send, small_recv, big_send, big_all,
    ids_send, ids_recv, big_marks, back_send, back_recv,
    in_sem, ids_ss, ids_rs, small_ss, small_rs, one_ss, one_rs, two_ss, two_rs,
    sback_ss, sback_rs, bback_ss, bback_rs,
):
    shards, blocks, cs, cb = dims
    n = shards * blocks
    rows = pooled.shape[0]
    nb = back_recv.shape[0]
    limit = BIG_OWN * shards
    me_d, me_b = lax.axis_index("docs"), lax.axis_index("blk")
    me = me_b * shards + me_d
    group = blocks * cb
    offsets = [blocks // 2] + [j for j in range(blocks) if j not in (0, blocks // 2)] + [0]
    peers = []
    for boff in offsets:
        for doff in range(shards - 1, -1, -1):
            if (boff, doff) != (0, 0):
                b, d = lax.rem(me_b + boff, blocks), lax.rem(me_d + doff, shards)
                peers.append((boff, d, b, b * shards + d))
    line = [lax.rem(me_b + boff, blocks) for boff in offsets if boff]
    cross = [lax.rem(me_d + doff, shards) for doff in range(1, shards)]

    load_rows = pltpu.make_async_copy(pooled_hbm, pooled, in_sem.at[0])
    load_weight = pltpu.make_async_copy(weight_hbm, weight, in_sem.at[1])
    load_rows.start()
    load_weight.start()
    barrier = pltpu.get_barrier_semaphore()
    for _, d, b, q in peers:
        pl.semaphore_signal(barrier, inc=1, device_id={"docs": d, "blk": b}, device_id_type=MESH)

    def copy(src, dst, ssem, rsem, d, b):
        return pltpu.make_async_remote_copy(
            src_ref=src, dst_ref=dst, send_sem=ssem, recv_sem=rsem,
            device_id={"docs": d, "blk": b}, device_id_type=MESH,
        )

    def ids_copy(to, slot, d, b):
        return copy(ids_send.at[to], ids_recv.at[slot], ids_ss.at[to], ids_rs.at[slot], d, b)

    def rows_at(ref, index, size):
        return ref.at[pl.ds(pl.multiple_of(index * size, 16), size)]

    def small_copy(to, slot, d, b):
        return copy(rows_at(small_send, to, cs), rows_at(small_recv, slot, cs), small_ss.at[to], small_rs.at[slot], d, b)

    def one_copy(to, slot, d, b):
        return copy(rows_at(big_send, to, cb), rows_at(big_all, me_d * blocks + slot, cb), one_ss.at[to], one_rs.at[slot], d, b)

    def two_copy(to, slot, d, b):
        return copy(rows_at(big_all, me_d, group), rows_at(big_all, slot, group), two_ss.at[to], two_rs.at[slot], d, b)

    def sback_copy(to, slot, d, b):
        return copy(back_send.at[to], back_recv.at[slot], sback_ss.at[to], sback_rs.at[slot], d, b)

    def bback_copy(to, slot, d, b):
        return copy(back_send.at[n + to], back_recv.at[n + slot], bback_ss.at[to], bback_rs.at[slot], d, b)

    cluster = cluster_ref[...]
    is_big = cluster < limit
    lane_rest = cluster - limit
    bucket = jnp.where(is_big, n + lax.rem(cluster, blocks), lax.rem(jnp.maximum(lane_rest, 0), n))
    local_id = jnp.where(is_big, cluster // blocks, jnp.maximum(lane_rest, 0) // n) + 1
    onehot = iota((nb, rows), 0) == bucket
    before = jnp.dot(
        onehot.astype(BF16), (iota((rows, rows), 0) < iota((rows, rows), 1)).astype(BF16),
        preferred_element_type=F32,
    )
    rank = jnp.sum(jnp.where(onehot, before, 0.0), axis=0, keepdims=True).astype(jnp.int32)
    at_rank = iota((LANES, rows), 0) == rank
    ids = nt(jnp.where(onehot, local_id.astype(F32), 0.0).astype(BF16), at_rank.astype(BF16))
    first = iota((8, LANES), 0) == 0
    for q in range(n):
        g = n + q // shards
        ids_send[q] = jnp.where(
            first, jnp.broadcast_to(ids[q : q + 1], (8, LANES)), jnp.broadcast_to(ids[g : g + 1], (8, LANES))
        )
    ids_recv[me] = ids_send[me]
    for q in range(n + blocks, nb):
        back_recv[q] = jnp.zeros((8, LANES), F32)

    load_rows.wait()
    load_weight.wait()
    projected = jnp.dot(pooled[...], weight[...], preferred_element_type=F32)
    norm = jnp.sqrt(jnp.sum(projected * projected, axis=1, keepdims=True) + 1e-06)
    embedded[...] = (projected / norm).astype(BF16)
    big_slot = jnp.where(is_big, (bucket - n) * cb + rank, -1)
    pick = (iota((group, rows), 0) == big_slot).astype(BF16)
    big_send[...] = jnp.dot(pick, embedded[...], preferred_element_type=F32).astype(BF16)

    pl.semaphore_wait(barrier, n - 1)
    for b in line:
        one_copy(b, me_b, me_d, b).start()
    for _, d, b, q in peers:
        ids_copy(q, me, d, b).start()
    own = pl.ds(pl.multiple_of((me_d * blocks + me_b) * cb, 16), cb)
    big_all[own, :] = big_send[pl.ds(pl.multiple_of(me_b * cb, 16), cb), :]

    span = shards * cs
    small_slot = jnp.where(is_big, -1, bucket * cs + rank)
    for boff in offsets:
        b = lax.rem(me_b + boff, blocks)
        pick = (iota((span, rows), 0) + b * span == small_slot).astype(BF16)
        small_send[pl.ds(pl.multiple_of(b * span, 16), span), :] = jnp.dot(
            pick, embedded[...], preferred_element_type=F32
        ).astype(BF16)
        for at, d, b2, q in peers:
            if at == boff:
                small_copy(q, me, d, b2).start()
    own = pl.ds(pl.multiple_of(me * cs, 16), cs)
    small_recv[own, :] = small_send[own, :]

    for b in line:
        one_copy(b, b, me_d, b).wait_recv()
    for d in cross:
        two_copy(d, me_d, d, me_b).start()

    for _, d, b, q in peers:
        ids_copy(q, q, d, b).wait_recv()
    total = n * cs
    low = iota((total, n), 1) * cs
    at = iota((total, n), 0)
    inside = (at >= low) & (at < low + cs)
    base = jnp.sum(jnp.where(inside, low, 0).astype(F32), axis=1, keepdims=True).astype(jnp.int32)
    small_lane = iota((total, LANES), 1) == iota((total, LANES), 0) - base
    marks = jnp.dot(inside.astype(BF16), ids_recv[:, 0, :].astype(BF16), preferred_element_type=F32)
    marks = jnp.where(small_lane, marks, 0.0)
    small_col = jnp.sum(marks, axis=1, keepdims=True)
    small_row = nt(jnp.ones((8, LANES), BF16), marks.astype(BF16))[0:1]

    big_total = n * cb
    source = iota((big_total, n), 1)
    low = (lax.rem(source, shards) * blocks + source // shards) * cb
    at = iota((big_total, n), 0)
    inside = (at >= low) & (at < low + cb)
    base = jnp.sum(jnp.where(inside, low, 0).astype(F32), axis=1, keepdims=True).astype(jnp.int32)
    marks = jnp.dot(inside.astype(BF16), ids_recv[:, 1, :].astype(BF16), preferred_element_type=F32)
    big_marks[...] = jnp.where(iota((big_total, LANES), 1) == iota((big_total, LANES), 0) - base, marks, 0.0)

    mine = pl.ds(pl.multiple_of(me_d * group, 16), group)
    my_row = nt(jnp.ones((8, LANES), BF16), big_marks[mine, :].astype(BF16))[0:1]
    best = jnp.full((1, group), -1.0, F32)
    for d in [me_d] + cross:
        if d is not me_d:
            two_copy(d, d, d, me_b).wait_recv()
        theirs = pl.ds(pl.multiple_of(d * group, 16), group)
        scores = nt(big_all[theirs, :], big_all[mine, :])
        allowed = jnp.sum(big_marks[theirs, :], axis=1, keepdims=True) == my_row
        if d is me_d:
            allowed = allowed & (iota((group, group), 0) != iota((group, group), 1))
        best = jnp.maximum(best, jnp.max(jnp.where(allowed, scores, -1.0), axis=0, keepdims=True))
    low = iota((blocks, group), 0) * cb
    at = iota((blocks, group), 1)
    spread = jnp.where((at >= low) & (at < low + cb), best, 0.0)
    place = lax.rem(iota((group, LANES), 0), cb) == iota((group, LANES), 1)
    back = exact_dot(spread, place.astype(F32))
    for b in range(blocks):
        back_send[n + b] = jnp.broadcast_to(back[b : b + 1], (8, LANES))
    for b in line:
        bback_copy(b, me_b, me_d, b).start()
    back_recv[n + me_b] = back_send[n + me_b]

    for _, d, b, q in peers:
        small_copy(q, q, d, b).wait_recv()
    width = next(w for w in (256, 128, total) if total % w == 0)
    parts = []
    for start in range(0, total, width):
        scores = nt(small_recv[...], small_recv[start : start + width, :])
        allowed = (small_col == small_row[:, start : start + width]) & (
            iota((total, width), 0) != iota((total, width), 1) + start
        )
        parts.append(jnp.max(jnp.where(allowed, scores, -1.0), axis=0, keepdims=True))
    best = jnp.concatenate(parts, axis=1) if len(parts) > 1 else parts[0]
    low = iota((n, total), 0) * cs
    at = iota((n, total), 1)
    spread = jnp.where((at >= low) & (at < low + cs), best, 0.0)
    back = exact_dot(spread, small_lane.astype(F32))
    for q in range(n):
        back_send[q] = jnp.broadcast_to(back[q : q + 1], (8, LANES))
    for _, d, b, q in peers:
        sback_copy(q, me, d, b).start()
    back_recv[me] = back_send[me]

    for b in line:
        bback_copy(b, b, me_d, b).wait_recv()
    for _, d, b, q in peers:
        sback_copy(q, q, d, b).wait_recv()
    result = exact_dot(back_recv[:, 0, :], at_rank.astype(F32))
    out_ref[...] = jnp.sum(jnp.where(onehot, result, 0.0), axis=0, keepdims=True)

    for b in line:
        one_copy(b, me_b, me_d, b).wait_send()
        bback_copy(b, me_b, me_d, b).wait_send()
    for d in cross:
        two_copy(d, me_d, d, me_b).wait_send()
    for _, d, b, q in peers:
        ids_copy(q, me, d, b).wait_send()
        small_copy(q, me, d, b).wait_send()
        sback_copy(q, me, d, b).wait_send()


def solution(mesh):
    shards, blocks = mesh.shape["docs"], mesh.shape["blk"]
    n = shards * blocks

    def body(pooled, proj_weight, cluster):
        rows, width = pooled.shape
        feature = proj_weight.shape[1]
        big_count = rows // 4
        cap_big = 2 * big_count // shards
        cap_small = 2 * (rows - big_count) // n
        cs = up(cap_small, 16)
        cb = up(cap_big * (shards // blocks), 16)
        nb = up(n + blocks, 16)
        dma = pltpu.SemaphoreType.DMA
        out = pl.pallas_call(
            functools.partial(kernel, (shards, blocks, cs, cb)),
            out_shape=jax.ShapeDtypeStruct((1, rows), F32),
            in_specs=[
                pl.BlockSpec(memory_space=pl.ANY),
                pl.BlockSpec(memory_space=pl.ANY),
                pl.BlockSpec(memory_space=pltpu.VMEM),
            ],
            out_specs=pl.BlockSpec(memory_space=pltpu.VMEM),
            scratch_shapes=[
                pltpu.VMEM((rows, width), BF16),
                pltpu.VMEM((width, feature), BF16),
                pltpu.VMEM((rows, feature), BF16),
                pltpu.VMEM((n * cs, feature), BF16),
                pltpu.VMEM((n * cs, feature), BF16),
                pltpu.VMEM((blocks * cb, feature), BF16),
                pltpu.VMEM((n * cb, feature), BF16),
                pltpu.VMEM((n, 8, LANES), F32),
                pltpu.VMEM((n, 8, LANES), F32),
                pltpu.VMEM((n * cb, LANES), F32),
                pltpu.VMEM((n + blocks, 8, LANES), F32),
                pltpu.VMEM((nb, 8, LANES), F32),
                dma((2,)), dma((n,)), dma((n,)), dma((n,)), dma((n,)), dma((blocks,)), dma((blocks,)),
                dma((shards,)), dma((shards,)), dma((n,)), dma((n,)), dma((blocks,)), dma((blocks,)),
            ],
            compiler_params=pltpu.CompilerParams(
                collective_id=0, has_side_effects=True, vmem_limit_bytes=60 * 1024 * 1024
            ),
        )(pooled, proj_weight, cluster.reshape(1, rows))
        return out.reshape(rows)

    in_specs = (P(("slab", "docs", "blk"), None), P(), P(("slab", "docs", "blk")))
    out_specs = P(("slab", "docs", "blk"))
    return jax.shard_map(body, mesh=mesh, in_specs=in_specs, out_specs=out_specs, check_vma=False)
```

```python
import functools

import jax
import jax.numpy as jnp
from jax import lax
from jax.experimental import pallas as pl
from jax.experimental.pallas import tpu as pltpu
from jax.sharding import PartitionSpec as P

MESH = pl.DeviceIdType.MESH
BIG_OWN = 4
LANES = 128
F32 = jnp.float32
BF16 = jnp.bfloat16


def up(value, step):
    return -(-value // step) * step


def iota(shape, dim):
    return lax.broadcasted_iota(jnp.int32, shape, dim)


def nt(a, b):
    return lax.dot_general(a, b, (((1,), (1,)), ((), ())), preferred_element_type=F32)


def exact_dot(a, b):
    return jnp.dot(a, b, preferred_element_type=F32, precision=lax.Precision.HIGHEST)


def kernel(
    dims, pooled_hbm, weight_hbm, cluster_ref, out_ref,
    pooled, weight, embedded, small_send, relay, small_recv, big_send, big_all,
    ids_send, ids_recv, big_marks, back_send, back_recv,
    in_sem, ids_ss, ids_rs, side_ss, side_rs, small_ss, small_rs, one_ss, one_rs, two_ss, two_rs,
    sback_ss, sback_rs, bback_ss, bback_rs,
):
    shards, blocks, cs, cb = dims
    n = shards * blocks
    rows = pooled.shape[0]
    nb = back_recv.shape[0]
    limit = BIG_OWN * shards
    cores = 2 if shards % 2 == 0 else 1
    chips = shards // cores
    me_d, me_b = lax.axis_index("docs"), lax.axis_index("blk")
    me_x, me_c = me_d // cores, lax.rem(me_d, cores)
    group = blocks * cb
    far = [blocks // 2] + [j for j in range(1, blocks) if j != blocks // 2]

    def docs_at(r, sign=1):
        dx, dc = r // cores, r % cores
        return lax.rem(me_x + sign * dx + chips, chips) * cores + lax.rem(me_c + dc, cores)

    def blk_at(j, sign=1):
        return lax.rem(me_b + sign * j + blocks, blocks)

    peers = [(r * blocks + j, r, j) for j in far + [0] for r in range(shards - 1, -1, -1) if (r, j) != (0, 0)]

    load_rows = pltpu.make_async_copy(pooled_hbm, pooled, in_sem.at[0])
    load_weight = pltpu.make_async_copy(weight_hbm, weight, in_sem.at[1])
    load_rows.start()
    load_weight.start()
    barrier = pltpu.get_barrier_semaphore()
    for _, r, j in peers:
        pl.semaphore_signal(
            barrier, inc=1, device_id={"docs": docs_at(r), "blk": blk_at(j)}, device_id_type=MESH
        )

    def copy(src, dst, ssem, rsem, d, b):
        return pltpu.make_async_remote_copy(
            src_ref=src, dst_ref=dst, send_sem=ssem, recv_sem=rsem,
            device_id={"docs": d, "blk": b}, device_id_type=MESH,
        )

    def chunk(ref, index, size):
        return ref.at[pl.ds(index * size, size)]

    def ids_copy(q, r, j):
        return copy(ids_send.at[q], ids_recv.at[q], ids_ss.at[q], ids_rs.at[q], docs_at(r), blk_at(j))

    def side_copy(r, j):
        q = r * blocks + j
        into = small_recv if j == 0 else relay
        return copy(chunk(small_send, q, cs), chunk(into, q, cs), side_ss.at[q], side_rs.at[q], docs_at(r), me_b)

    def line_copy(r, j):
        q = r * blocks + j
        return copy(chunk(relay, q, cs), chunk(small_recv, q, cs), small_ss.at[q], small_rs.at[q], me_d, blk_at(j))

    def one_copy(j):
        return copy(chunk(big_send, j, cb), chunk(big_all, j, cb), one_ss.at[j], one_rs.at[j], me_d, blk_at(j))

    def two_copy(r):
        if r == 1 or r % cores == 0:
            return copy(chunk(big_all, 0, group), chunk(big_all, r, group), two_ss.at[r], two_rs.at[r], docs_at(r), me_b)
        return copy(
            chunk(big_all, r - 1, group), chunk(big_all, r, group), two_ss.at[r], two_rs.at[r], docs_at(1), me_b
        )

    def sback_copy(q, r, j):
        return copy(
            back_send.at[q], back_recv.at[q], sback_ss.at[q], sback_rs.at[q], docs_at(r, -1), blk_at(j, -1)
        )

    def bback_copy(j):
        return copy(back_send.at[n + j], back_recv.at[n + j], bback_ss.at[j], bback_rs.at[j], me_d, blk_at(j, -1))

    cluster = cluster_ref[...]
    is_big = cluster < limit
    rest = jnp.maximum(cluster - limit, 0)
    owner = lax.rem(rest, n)
    owner_b, owner_d = owner // shards, lax.rem(owner, shards)
    side = lax.rem(owner_d // cores - me_x + chips, chips) * cores + lax.rem(lax.rem(owner_d, cores) - me_c + cores, cores)
    small_bucket = side * blocks + lax.rem(owner_b - me_b + blocks, blocks)
    big_bucket = n + lax.rem(lax.rem(cluster, blocks) - me_b + blocks, blocks)
    bucket = jnp.where(is_big, big_bucket, small_bucket)
    local_id = jnp.where(is_big, cluster // blocks, rest // n) + 1
    onehot = iota((nb, rows), 0) == bucket
    before = jnp.dot(
        onehot.astype(BF16), (iota((rows, rows), 0) < iota((rows, rows), 1)).astype(BF16),
        preferred_element_type=F32,
    )
    rank = jnp.sum(jnp.where(onehot, before, 0.0), axis=0, keepdims=True).astype(jnp.int32)
    at_rank = iota((LANES, rows), 0) == rank
    ids = nt(jnp.where(onehot, local_id.astype(F32), 0.0).astype(BF16), at_rank.astype(BF16))
    first = iota((8, LANES), 0) == 0
    for q in range(n):
        g = n + q % blocks
        ids_send[q] = jnp.where(
            first, jnp.broadcast_to(ids[q : q + 1], (8, LANES)), jnp.broadcast_to(ids[g : g + 1], (8, LANES))
        )
    ids_recv[0] = ids_send[0]
    for q in range(n + blocks, nb):
        back_recv[q] = jnp.zeros((8, LANES), F32)

    load_rows.wait()
    load_weight.wait()
    projected = jnp.dot(pooled[...], weight[...], preferred_element_type=F32)
    norm = jnp.sqrt(jnp.sum(projected * projected, axis=1, keepdims=True) + 1e-06)
    embedded[...] = (projected / norm).astype(BF16)
    big_slot = jnp.where(is_big, (bucket - n) * cb + rank, -1)
    pick = (iota((group, rows), 0) == big_slot).astype(BF16)
    big_send[...] = jnp.dot(pick, embedded[...], preferred_element_type=F32).astype(BF16)

    pl.semaphore_wait(barrier, n - 1)
    for j in far:
        one_copy(j).start()
    for q, r, j in peers:
        ids_copy(q, r, j).start()
    big_all[0:cb, :] = big_send[0:cb, :]

    small_slot = jnp.where(is_big, -1, bucket * cs + rank)
    order = [r for r in range(cores, shards)] + [r for r in range(1, cores)] + [0]
    span = blocks * cs
    for r in order:
        pick = (iota((span, rows), 0) + r * span == small_slot).astype(BF16)
        picked = jnp.dot(pick, embedded[...], preferred_element_type=F32).astype(BF16)
        if r:
            small_send[r * span : (r + 1) * span, :] = picked
        else:
            relay[0:span, :] = picked
            small_recv[0:cs, :] = picked[0:cs]
        for j in far + [0]:
            if r:
                side_copy(r, j).start()
            elif j:
                line_copy(r, j).start()

    for r in range(1, shards):
        if r == cores:
            for j in far:
                one_copy(j).wait_recv()
            for r2 in range(1, shards):
                if r2 == 1 or r2 % cores == 0:
                    two_copy(r2).start()
        for j in far:
            side_copy(r, j).wait_recv()
            line_copy(r, j).start()

    for q, r, j in peers:
        ids_copy(q, r, j).wait_recv()
    total = n * cs
    low = iota((total, n), 1) * cs
    at = iota((total, n), 0)
    inside = (at >= low) & (at < low + cs)
    base = jnp.sum(jnp.where(inside, low, 0).astype(F32), axis=1, keepdims=True).astype(jnp.int32)
    small_lane = iota((total, LANES), 1) == iota((total, LANES), 0) - base
    marks = jnp.dot(inside.astype(BF16), ids_recv[:, 0, :].astype(BF16), preferred_element_type=F32)
    marks = jnp.where(small_lane, marks, 0.0)
    small_col = jnp.sum(marks, axis=1, keepdims=True)
    small_row = nt(jnp.ones((8, LANES), BF16), marks.astype(BF16))[0:1]

    big_total = n * cb
    low = iota((big_total, n), 1) * cb
    at = iota((big_total, n), 0)
    inside = (at >= low) & (at < low + cb)
    base = jnp.sum(jnp.where(inside, low, 0).astype(F32), axis=1, keepdims=True).astype(jnp.int32)
    marks = jnp.dot(inside.astype(BF16), ids_recv[:, 1, :].astype(BF16), preferred_element_type=F32)
    big_marks[...] = jnp.where(iota((big_total, LANES), 1) == iota((big_total, LANES), 0) - base, marks, 0.0)

    my_row = nt(jnp.ones((8, LANES), BF16), big_marks[0:group, :].astype(BF16))[0:1]
    best = jnp.full((1, group), -1.0, F32)
    for r in range(shards):
        if r:
            two_copy(r).wait_recv()
            if r % cores == 0 and cores > 1:
                two_copy(r + 1).start()
        theirs = pl.ds(r * group, group)
        scores = nt(big_all[theirs, :], big_all[0:group, :])
        allowed = jnp.sum(big_marks[theirs, :], axis=1, keepdims=True) == my_row
        if r == 0:
            allowed = allowed & (iota((group, group), 0) != iota((group, group), 1))
        best = jnp.maximum(best, jnp.max(jnp.where(allowed, scores, -1.0), axis=0, keepdims=True))
    low = iota((blocks, group), 0) * cb
    at = iota((blocks, group), 1)
    spread = jnp.where((at >= low) & (at < low + cb), best, 0.0)
    place = lax.rem(iota((group, LANES), 0), cb) == iota((group, LANES), 1)
    back = exact_dot(spread, place.astype(F32))
    for b in range(blocks):
        back_send[n + b] = jnp.broadcast_to(back[b : b + 1], (8, LANES))
    for j in far:
        bback_copy(j).start()
    back_recv[n] = back_send[n]

    for q, r, j in peers:
        (line_copy if j else side_copy)(r, j).wait_recv()
    width = next(w for w in (256, 128, total) if total % w == 0)
    parts = []
    for start in range(0, total, width):
        scores = nt(small_recv[...], small_recv[start : start + width, :])
        allowed = (small_col == small_row[:, start : start + width]) & (
            iota((total, width), 0) != iota((total, width), 1) + start
        )
        parts.append(jnp.max(jnp.where(allowed, scores, -1.0), axis=0, keepdims=True))
    best = jnp.concatenate(parts, axis=1) if len(parts) > 1 else parts[0]
    low = iota((n, total), 0) * cs
    at = iota((n, total), 1)
    spread = jnp.where((at >= low) & (at < low + cs), best, 0.0)
    back = exact_dot(spread, small_lane.astype(F32))
    for q in range(n):
        back_send[q] = jnp.broadcast_to(back[q : q + 1], (8, LANES))
    for q, r, j in peers:
        sback_copy(q, r, j).start()
    back_recv[0] = back_send[0]

    for j in far:
        bback_copy(j).wait_recv()
    for q, r, j in peers:
        sback_copy(q, r, j).wait_recv()
    result = exact_dot(back_recv[:, 0, :], at_rank.astype(F32))
    out_ref[...] = jnp.sum(jnp.where(onehot, result, 0.0), axis=0, keepdims=True)

    for j in far:
        one_copy(j).wait_send()
        bback_copy(j).wait_send()
    for r in range(1, shards):
        two_copy(r).wait_send()
    for q, r, j in peers:
        ids_copy(q, r, j).wait_send()
        sback_copy(q, r, j).wait_send()
        if r:
            side_copy(r, j).wait_send()
        if j:
            line_copy(r, j).wait_send()


def solution(mesh):
    shards, blocks = mesh.shape["docs"], mesh.shape["blk"]
    n = shards * blocks

    def body(pooled, proj_weight, cluster):
        rows, width = pooled.shape
        feature = proj_weight.shape[1]
        big_count = rows // 4
        cap_big = 2 * big_count // shards
        cap_small = 2 * (rows - big_count) // n
        cs = up(cap_small, 16)
        cb = up(cap_big * (shards // blocks), 16)
        nb = up(n + blocks, 16)
        dma = pltpu.SemaphoreType.DMA
        out = pl.pallas_call(
            functools.partial(kernel, (shards, blocks, cs, cb)),
            out_shape=jax.ShapeDtypeStruct((1, rows), F32),
            in_specs=[
                pl.BlockSpec(memory_space=pl.ANY),
                pl.BlockSpec(memory_space=pl.ANY),
                pl.BlockSpec(memory_space=pltpu.VMEM),
            ],
            out_specs=pl.BlockSpec(memory_space=pltpu.VMEM),
            scratch_shapes=[
                pltpu.VMEM((rows, width), BF16),
                pltpu.VMEM((width, feature), BF16),
                pltpu.VMEM((rows, feature), BF16),
                pltpu.VMEM((n * cs, feature), BF16),
                pltpu.VMEM((n * cs, feature), BF16),
                pltpu.VMEM((n * cs, feature), BF16),
                pltpu.VMEM((blocks * cb, feature), BF16),
                pltpu.VMEM((n * cb, feature), BF16),
                pltpu.VMEM((n, 8, LANES), F32),
                pltpu.VMEM((n, 8, LANES), F32),
                pltpu.VMEM((n * cb, LANES), F32),
                pltpu.VMEM((n + blocks, 8, LANES), F32),
                pltpu.VMEM((nb, 8, LANES), F32),
                dma((2,)), dma((n,)), dma((n,)), dma((n,)), dma((n,)), dma((n,)), dma((n,)), dma((blocks,)), dma((blocks,)),
                dma((shards,)), dma((shards,)), dma((n,)), dma((n,)), dma((blocks,)), dma((blocks,)),
            ],
            compiler_params=pltpu.CompilerParams(
                collective_id=0, has_side_effects=True, vmem_limit_bytes=60 * 1024 * 1024
            ),
        )(pooled, proj_weight, cluster.reshape(1, rows))
        return out.reshape(rows)

    in_specs = (P(("slab", "docs", "blk"), None), P(), P(("slab", "docs", "blk")))
    out_specs = P(("slab", "docs", "blk"))
    return jax.shard_map(body, mesh=mesh, in_specs=in_specs, out_specs=out_specs, check_vma=False)
```

```python
import functools

import jax
import jax.numpy as jnp
from jax import lax
from jax.experimental import pallas as pl
from jax.experimental.pallas import tpu as pltpu
from jax.sharding import PartitionSpec as P

MESH = pl.DeviceIdType.MESH
BIG_OWN = 4
LANES = 128
F32 = jnp.float32
BF16 = jnp.bfloat16


def up(value, step):
    return -(-value // step) * step


def iota(shape, dim):
    return lax.broadcasted_iota(jnp.int32, shape, dim)


def nt(a, b):
    return lax.dot_general(a, b, (((1,), (1,)), ((), ())), preferred_element_type=F32)


def exact_dot(a, b):
    high = a.astype(BF16)
    rest = a - high.astype(F32)
    middle = rest.astype(BF16)
    low = (rest - middle.astype(F32)).astype(BF16)
    three = jnp.dot(jnp.concatenate([high, middle, low], axis=0), b.astype(BF16), preferred_element_type=F32)
    m = a.shape[0]
    return three[:m] + three[m : 2 * m] + three[2 * m :]


def kernel(
    dims, pooled_hbm, weight_hbm, cluster_ref, out_ref,
    pooled, weight, embedded, small_send, relay, small_recv, big_send, big_all,
    ids_send, ids_recv, big_marks, back_send, back_recv,
    in_sem, ids_ss, ids_rs, side_ss, side_rs, small_ss, small_rs, one_ss, one_rs, two_ss, two_rs,
    sback_ss, sback_rs, bback_ss, bback_rs,
):
    shards, blocks, cs, cb = dims
    n = shards * blocks
    rows = pooled.shape[0]
    nb = back_recv.shape[0]
    limit = BIG_OWN * shards
    cores = 2 if shards % 2 == 0 else 1
    chips = shards // cores
    me_d, me_b = lax.axis_index("docs"), lax.axis_index("blk")
    me_x, me_c = me_d // cores, lax.rem(me_d, cores)
    group = blocks * cb
    far = [blocks // 2] + [j for j in range(1, blocks) if j != blocks // 2]
    steps = far

    def docs_at(r, sign=1):
        dx, dc = r // cores, r % cores
        return lax.rem(me_x + sign * dx + chips, chips) * cores + lax.rem(me_c + dc, cores)

    def blk_at(j, sign=1):
        return lax.rem(me_b + sign * j + blocks, blocks)

    peers = [(r * blocks + j, r, j) for j in far + [0] for r in range(shards - 1, -1, -1) if (r, j) != (0, 0)]

    load_rows = pltpu.make_async_copy(pooled_hbm, pooled, in_sem.at[0])
    load_weight = pltpu.make_async_copy(weight_hbm, weight, in_sem.at[1])
    load_rows.start()
    load_weight.start()
    barrier = pltpu.get_barrier_semaphore()
    for _, r, j in peers:
        pl.semaphore_signal(
            barrier, inc=1, device_id={"docs": docs_at(r), "blk": blk_at(j)}, device_id_type=MESH
        )

    def copy(src, dst, ssem, rsem, d, b):
        return pltpu.make_async_remote_copy(
            src_ref=src, dst_ref=dst, send_sem=ssem, recv_sem=rsem,
            device_id={"docs": d, "blk": b}, device_id_type=MESH,
        )

    def chunk(ref, index, size):
        return ref.at[pl.ds(index * size, size)]

    def ids_copy(q, r, j):
        return copy(ids_send.at[q], ids_recv.at[q], ids_ss.at[q], ids_rs.at[q], docs_at(r), blk_at(j))

    def side_copy(r, j):
        q = r * blocks + j
        into = small_recv if isinstance(j, int) and j == 0 else relay
        return copy(chunk(small_send, q, cs), chunk(into, q, cs), side_ss.at[q], side_rs.at[q], docs_at(r), me_b)

    def line_copy(r, j):
        q = r * blocks + j
        return copy(chunk(relay, q, cs), chunk(small_recv, q, cs), small_ss.at[q], small_rs.at[q], me_d, blk_at(j))

    def one_copy(j):
        return copy(chunk(big_send, j, cb), chunk(big_all, j, cb), one_ss.at[j], one_rs.at[j], me_d, blk_at(j))

    def two_copy(r):
        if r == 1 or r % cores == 0:
            return copy(chunk(big_all, 0, group), chunk(big_all, r, group), two_ss.at[r], two_rs.at[r], docs_at(r), me_b)
        return copy(
            chunk(big_all, r - 1, group), chunk(big_all, r, group), two_ss.at[r], two_rs.at[r], docs_at(1), me_b
        )

    def sback_copy(q, r, j):
        return copy(
            back_send.at[q], back_recv.at[q], sback_ss.at[q], sback_rs.at[q], docs_at(r, -1), blk_at(j, -1)
        )

    def bback_copy(j):
        return copy(back_send.at[n + j], back_recv.at[n + j], bback_ss.at[j], bback_rs.at[j], me_d, blk_at(j, -1))

    cluster = cluster_ref[...]
    is_big = cluster < limit
    rest = jnp.maximum(cluster - limit, 0)
    owner = lax.rem(rest, n)
    owner_b, owner_d = owner // shards, lax.rem(owner, shards)
    side = lax.rem(owner_d // cores - me_x + chips, chips) * cores + lax.rem(lax.rem(owner_d, cores) - me_c + cores, cores)
    small_bucket = side * blocks + lax.rem(owner_b - me_b + blocks, blocks)
    big_bucket = n + lax.rem(lax.rem(cluster, blocks) - me_b + blocks, blocks)
    bucket = jnp.where(is_big, big_bucket, small_bucket)
    local_id = jnp.where(is_big, cluster // blocks, rest // n) + 1
    onehot = iota((nb, rows), 0) == bucket
    before = jnp.dot(
        onehot.astype(BF16), (iota((rows, rows), 0) < iota((rows, rows), 1)).astype(BF16),
        preferred_element_type=F32,
    )
    rank = jnp.sum(jnp.where(onehot, before, 0.0), axis=0, keepdims=True).astype(jnp.int32)
    at_rank = iota((LANES, rows), 0) == rank
    ids = nt(jnp.where(onehot, local_id.astype(F32), 0.0).astype(BF16), at_rank.astype(BF16))
    for q in range(n):
        g = n + q % blocks
        ids_send[q] = jnp.concatenate([ids[q : q + 1], ids[g : g + 1]], axis=1)
    ids_recv[0] = ids_send[0]
    for q in range(n + blocks, nb):
        back_recv[q] = jnp.zeros((1, LANES), F32)

    load_rows.wait()
    load_weight.wait()
    projected = jnp.dot(pooled[...], weight[...], preferred_element_type=F32)
    norm = jnp.sqrt(jnp.sum(projected * projected, axis=1, keepdims=True) + 1e-06)
    embedded[...] = (projected / norm).astype(BF16)
    big_slot = jnp.where(is_big, (bucket - n) * cb + rank, -1)
    pick = (iota((group, rows), 0) == big_slot).astype(BF16)
    big_send[...] = jnp.dot(pick, embedded[...], preferred_element_type=F32).astype(BF16)

    big_all[0:cb, :] = big_send[0:cb, :]

    small_slot = jnp.where(is_big, -1, bucket * cs + rank)
    order = [r for r in range(cores, shards)] + [r for r in range(1, cores)] + [0]
    span = blocks * cs
    for r in order:
        pick = (iota((span, rows), 0) + r * span == small_slot).astype(BF16)
        picked = jnp.dot(pick, embedded[...], preferred_element_type=F32).astype(BF16)
        if r:
            small_send[r * span : (r + 1) * span, :] = picked
        else:
            relay[0:span, :] = picked
            small_recv[0:cs, :] = picked[0:cs]

    pl.semaphore_wait(barrier, n - 1)
    for j in steps:
        one_copy(j).start()
    for q, r, j in peers:
        ids_copy(q, r, j).start()
    for r in order:
        for j in steps:
            (side_copy if r else line_copy)(r, j).start()
        if r:
            side_copy(r, 0).start()
    for r in range(1, shards):
        if r == cores:
            for j in far:
                one_copy(j).wait_recv()
            for r2 in range(1, shards):
                if r2 == 1 or r2 % cores == 0:
                    two_copy(r2).start()
        for j in steps:
            side_copy(r, j).wait_recv()
            line_copy(r, j).start()

    for q, r, j in peers:
        ids_copy(q, r, j).wait_recv()
    total = n * cs
    low = iota((total, n), 1) * cs
    at = iota((total, n), 0)
    inside = (at >= low) & (at < low + cs)
    base = jnp.sum(jnp.where(inside, low, 0).astype(F32), axis=1, keepdims=True).astype(jnp.int32)
    small_lane = iota((total, LANES), 1) == iota((total, LANES), 0) - base
    marks = jnp.dot(inside.astype(BF16), ids_recv[:, 0, 0:LANES].astype(BF16), preferred_element_type=F32)
    marks = jnp.where(small_lane, marks, 0.0)
    small_col = jnp.sum(marks, axis=1, keepdims=True)
    small_row = nt(jnp.ones((8, LANES), BF16), marks.astype(BF16))[0:1]

    big_total = n * cb
    low = iota((big_total, n), 1) * cb
    at = iota((big_total, n), 0)
    inside = (at >= low) & (at < low + cb)
    base = jnp.sum(jnp.where(inside, low, 0).astype(F32), axis=1, keepdims=True).astype(jnp.int32)
    marks = jnp.dot(inside.astype(BF16), ids_recv[:, 0, LANES:].astype(BF16), preferred_element_type=F32)
    big_marks[...] = jnp.where(iota((big_total, LANES), 1) == iota((big_total, LANES), 0) - base, marks, 0.0)

    my_row = nt(jnp.ones((8, LANES), BF16), big_marks[0:group, :].astype(BF16))[0:1]
    best = jnp.full((1, group), -1.0, F32)
    for r in range(shards):
        if r:
            two_copy(r).wait_recv()
            if r % cores == 0 and cores > 1:
                two_copy(r + 1).start()
        theirs = pl.ds(r * group, group)
        scores = nt(big_all[theirs, :], big_all[0:group, :])
        allowed = jnp.sum(big_marks[theirs, :], axis=1, keepdims=True) == my_row
        if r == 0:
            allowed = allowed & (iota((group, group), 0) != iota((group, group), 1))
        best = jnp.maximum(best, jnp.max(jnp.where(allowed, scores, -1.0), axis=0, keepdims=True))
    low = iota((up(blocks, 16), group), 0) * cb
    at = iota((up(blocks, 16), group), 1)
    spread = jnp.where((at >= low) & (at < low + cb), best, 0.0)
    place = lax.rem(iota((group, LANES), 0), cb) == iota((group, LANES), 1)
    back = exact_dot(spread, place.astype(F32))
    for b in range(blocks):
        back_send[n + b] = back[b : b + 1]
    for j in far:
        bback_copy(j).start()
    back_recv[n] = back_send[n]

    def small_best(r0, r1, c0, c1):
        scores = nt(small_recv[r0:r1, :], small_recv[c0:c1, :])
        allowed = small_col[r0:r1] == small_row[:, c0:c1]
        if r0 < c1 and c0 < r1:
            allowed = allowed & (iota((r1 - r0, c1 - c0), 0) + r0 != iota((r1 - r0, c1 - c0), 1) + c0)
        return jnp.max(jnp.where(allowed, scores, -1.0), axis=0, keepdims=True)

    width = next(w for w in (256, 128, total) if total % w == 0)
    cut = total - span
    parts = []
    for r in range(shards):
        if r == shards - 1:
            parts = [small_best(0, cut, c, c + width) for c in range(0, cut - width + 1, width)]
        for j in range(blocks):
            if (r, j) != (0, 0):
                (line_copy if j else side_copy)(r, j).wait_recv()
    for c in range(0, total, width):
        late = small_best(cut, total, c, c + width)
        if c // width < len(parts):
            parts[c // width] = jnp.maximum(parts[c // width], late)
        else:
            parts.append(jnp.maximum(small_best(0, cut, c, c + width), late))
    best = jnp.concatenate(parts, axis=1) if len(parts) > 1 else parts[0]
    low = iota((n, total), 0) * cs
    at = iota((n, total), 1)
    spread = jnp.where((at >= low) & (at < low + cs), best, 0.0)
    back = exact_dot(spread, small_lane.astype(F32))
    for q in range(n):
        back_send[q] = back[q : q + 1]
    for q, r, j in peers:
        sback_copy(q, r, j).start()
    back_recv[0] = back_send[0]

    for j in far:
        bback_copy(j).wait_recv()
    for q, r, j in peers:
        sback_copy(q, r, j).wait_recv()
    result = exact_dot(back_recv[:, 0, :], at_rank.astype(F32))
    out_ref[...] = jnp.sum(jnp.where(onehot, result, 0.0), axis=0, keepdims=True)

    for j in far:
        one_copy(j).wait_send()
        bback_copy(j).wait_send()
    for r in range(1, shards):
        two_copy(r).wait_send()
    for q, r, j in peers:
        ids_copy(q, r, j).wait_send()
        sback_copy(q, r, j).wait_send()
        if r:
            side_copy(r, j).wait_send()
        if j:
            line_copy(r, j).wait_send()


def solution(mesh):
    shards, blocks = mesh.shape["docs"], mesh.shape["blk"]
    n = shards * blocks

    def body(pooled, proj_weight, cluster):
        rows, width = pooled.shape
        feature = proj_weight.shape[1]
        big_count = rows // 4
        cap_big = 2 * big_count // shards
        cap_small = 2 * (rows - big_count) // n
        cs = up(cap_small, 16)
        cb = up(cap_big * (shards // blocks), 16)
        nb = up(n + blocks, 16)
        dma = pltpu.SemaphoreType.DMA
        out = pl.pallas_call(
            functools.partial(kernel, (shards, blocks, cs, cb)),
            out_shape=jax.ShapeDtypeStruct((1, rows), F32),
            in_specs=[
                pl.BlockSpec(memory_space=pl.ANY),
                pl.BlockSpec(memory_space=pl.ANY),
                pl.BlockSpec(memory_space=pltpu.VMEM),
            ],
            out_specs=pl.BlockSpec(memory_space=pltpu.VMEM),
            scratch_shapes=[
                pltpu.VMEM((rows, width), BF16),
                pltpu.VMEM((width, feature), BF16),
                pltpu.VMEM((rows, feature), BF16),
                pltpu.VMEM((n * cs, feature), BF16),
                pltpu.VMEM((n * cs, feature), BF16),
                pltpu.VMEM((n * cs, feature), BF16),
                pltpu.VMEM((blocks * cb, feature), BF16),
                pltpu.VMEM((n * cb, feature), BF16),
                pltpu.VMEM((n, 1, 2 * LANES), F32),
                pltpu.VMEM((n, 1, 2 * LANES), F32),
                pltpu.VMEM((n * cb, LANES), F32),
                pltpu.VMEM((n + blocks, 1, LANES), F32),
                pltpu.VMEM((nb, 1, LANES), F32),
                dma((2,)), dma((n,)), dma((n,)), dma((n,)), dma((n,)), dma((n,)), dma((n,)), dma((blocks,)), dma((blocks,)),
                dma((shards,)), dma((shards,)), dma((n,)), dma((n,)), dma((blocks,)), dma((blocks,)),
            ],
            compiler_params=pltpu.CompilerParams(
                collective_id=0, has_side_effects=True, vmem_limit_bytes=60 * 1024 * 1024
            ),
        )(pooled, proj_weight, cluster.reshape(1, rows))
        return jnp.maximum(out.reshape(rows), -1.0)

    in_specs = (P(("slab", "docs", "blk"), None), P(), P(("slab", "docs", "blk")))
    out_specs = P(("slab", "docs", "blk"))
    return jax.shard_map(body, mesh=mesh, in_specs=in_specs, out_specs=out_specs, check_vma=False)
```

```python
import functools

import jax
import jax.numpy as jnp
from jax import lax
from jax.experimental import pallas as pl
from jax.experimental.pallas import tpu as pltpu
from jax.sharding import PartitionSpec as P

MESH = pl.DeviceIdType.MESH
BIG_OWN = 4
LANES = 128
F32 = jnp.float32
BF16 = jnp.bfloat16


def up(value, step):
    return -(-value // step) * step


def iota(shape, dim):
    return lax.broadcasted_iota(jnp.int32, shape, dim)


def nt(a, b):
    return lax.dot_general(a, b, (((1,), (1,)), ((), ())), preferred_element_type=F32)


def exact_dot(a, b):
    high = a.astype(BF16)
    rest = a - high.astype(F32)
    middle = rest.astype(BF16)
    low = (rest - middle.astype(F32)).astype(BF16)
    three = jnp.dot(jnp.concatenate([high, middle, low], axis=0), b.astype(BF16), preferred_element_type=F32)
    m = a.shape[0]
    return three[:m] + three[m : 2 * m] + three[2 * m :]


def kernel(
    dims, pooled_hbm, weight_hbm, cluster_ref, out_ref,
    pooled, weight, embedded, small_send, relay, small_recv, big_send, big_all,
    ids_send, ids_recv, big_marks, back_send, back_recv,
    in_sem, ids_ss, ids_rs, side_ss, side_rs, small_ss, small_rs, one_ss, one_rs, two_ss, two_rs,
    sback_ss, sback_rs, bback_ss, bback_rs,
):
    shards, blocks, cs, cb = dims
    n = shards * blocks
    rows = pooled.shape[0]
    nb = back_recv.shape[0]
    limit = BIG_OWN * shards
    cores = 2 if shards % 2 == 0 else 1
    chips = shards // cores
    me_d, me_b = lax.axis_index("docs"), lax.axis_index("blk")
    me_x, me_c = me_d // cores, lax.rem(me_d, cores)
    group = blocks * cb
    far = [blocks // 2] + [j for j in range(1, blocks) if j != blocks // 2]
    steps = far

    def docs_at(r, sign=1):
        dx, dc = r // cores, r % cores
        return lax.rem(me_x + sign * dx + chips, chips) * cores + lax.rem(me_c + dc, cores)

    def blk_at(j, sign=1):
        return lax.rem(me_b + sign * j + blocks, blocks)

    peers = [(r * blocks + j, r, j) for j in far + [0] for r in range(shards - 1, -1, -1) if (r, j) != (0, 0)]

    load_rows = pltpu.make_async_copy(pooled_hbm, pooled, in_sem.at[0])
    load_weight = pltpu.make_async_copy(weight_hbm, weight, in_sem.at[1])
    load_rows.start()
    load_weight.start()
    barrier = pltpu.get_barrier_semaphore()
    for _, r, j in peers:
        pl.semaphore_signal(
            barrier, inc=1, device_id={"docs": docs_at(r), "blk": blk_at(j)}, device_id_type=MESH
        )

    def copy(src, dst, ssem, rsem, d, b):
        return pltpu.make_async_remote_copy(
            src_ref=src, dst_ref=dst, send_sem=ssem, recv_sem=rsem,
            device_id={"docs": d, "blk": b}, device_id_type=MESH,
        )

    def chunk(ref, index, size):
        return ref.at[pl.ds(index * size, size)]

    def ids_copy(q, r, j):
        return copy(ids_send.at[q], ids_recv.at[q], ids_ss.at[q], ids_rs.at[q], docs_at(r), blk_at(j))

    def side_copy(r, j):
        q = r * blocks + j
        into = small_recv if isinstance(j, int) and j == 0 else relay
        return copy(chunk(small_send, q, cs), chunk(into, q, cs), side_ss.at[q], side_rs.at[q], docs_at(r), me_b)

    def line_copy(r, j):
        q = r * blocks + j
        return copy(chunk(relay, q, cs), chunk(small_recv, q, cs), small_ss.at[q], small_rs.at[q], me_d, blk_at(j))

    def one_copy(j):
        return copy(chunk(big_send, j, cb), chunk(big_all, j, cb), one_ss.at[j], one_rs.at[j], me_d, blk_at(j))

    def two_copy(r):
        if r == 1 or r % cores == 0:
            return copy(chunk(big_all, 0, group), chunk(big_all, r, group), two_ss.at[r], two_rs.at[r], docs_at(r), me_b)
        return copy(
            chunk(big_all, r - 1, group), chunk(big_all, r, group), two_ss.at[r], two_rs.at[r], docs_at(1), me_b
        )

    def sback_copy(q, r, j):
        return copy(
            back_send.at[q], back_recv.at[q], sback_ss.at[q], sback_rs.at[q], docs_at(r, -1), blk_at(j, -1)
        )

    def bback_copy(j):
        return copy(back_send.at[n + j], back_recv.at[n + j], bback_ss.at[j], bback_rs.at[j], me_d, blk_at(j, -1))

    cluster = cluster_ref[...]
    is_big = cluster < limit
    rest = jnp.maximum(cluster - limit, 0)
    owner = lax.rem(rest, n)
    owner_b, owner_d = owner // shards, lax.rem(owner, shards)
    side = lax.rem(owner_d // cores - me_x + chips, chips) * cores + lax.rem(lax.rem(owner_d, cores) - me_c + cores, cores)
    small_bucket = side * blocks + lax.rem(owner_b - me_b + blocks, blocks)
    big_bucket = n + lax.rem(lax.rem(cluster, blocks) - me_b + blocks, blocks)
    bucket = jnp.where(is_big, big_bucket, small_bucket)
    local_id = jnp.where(is_big, cluster // blocks, rest // n) + 1
    onehot = iota((nb, rows), 0) == bucket
    before = jnp.dot(
        onehot.astype(BF16), (iota((rows, rows), 0) < iota((rows, rows), 1)).astype(BF16),
        preferred_element_type=F32,
    )
    rank = jnp.sum(jnp.where(onehot, before, 0.0), axis=0, keepdims=True).astype(jnp.int32)
    at_rank = iota((LANES, rows), 0) == rank
    ids = nt(jnp.where(onehot, local_id.astype(F32), 0.0).astype(BF16), at_rank.astype(BF16))
    for q in range(n):
        g = n + q % blocks
        ids_send[q] = jnp.concatenate([ids[q : q + 1], ids[g : g + 1]], axis=1)
    ids_recv[0] = ids_send[0]
    for q in range(n + blocks, nb):
        back_recv[q] = jnp.zeros((1, LANES), F32)

    load_rows.wait()
    load_weight.wait()
    projected = jnp.dot(pooled[...], weight[...], preferred_element_type=F32)
    norm = jnp.sqrt(jnp.sum(projected * projected, axis=1, keepdims=True) + 1e-06)
    embedded[...] = (projected / norm).astype(BF16)
    big_slot = jnp.where(is_big, (bucket - n) * cb + rank, -1)
    pick = (iota((group, rows), 0) == big_slot).astype(BF16)
    big_send[...] = jnp.dot(pick, embedded[...], preferred_element_type=F32).astype(BF16)

    big_all[0:cb, :] = big_send[0:cb, :]

    small_slot = jnp.where(is_big, -1, bucket * cs + rank)
    order = [r for r in range(cores, shards)] + [r for r in range(1, cores)] + [0]
    span = blocks * cs
    for r in order:
        pick = (iota((span, rows), 0) + r * span == small_slot).astype(BF16)
        picked = jnp.dot(pick, embedded[...], preferred_element_type=F32).astype(BF16)
        if r:
            small_send[r * span : (r + 1) * span, :] = picked
        else:
            relay[0:span, :] = picked
            small_recv[0:cs, :] = picked[0:cs]

    pl.semaphore_wait(barrier, n - 1)
    for j in steps:
        one_copy(j).start()
    for q, r, j in peers:
        ids_copy(q, r, j).start()
    for r in order:
        for j in steps:
            (side_copy if r else line_copy)(r, j).start()
        if r:
            side_copy(r, 0).start()
    for r in range(1, shards):
        if r == shards - 1:
            for j in far:
                one_copy(j).wait_recv()
            for r2 in range(1, shards):
                if r2 == 1 or r2 % cores == 0:
                    two_copy(r2).start()
        for j in steps:
            side_copy(r, j).wait_recv()
            line_copy(r, j).start()

    for q, r, j in peers:
        ids_copy(q, r, j).wait_recv()
    total = n * cs
    low = iota((total, n), 1) * cs
    at = iota((total, n), 0)
    inside = (at >= low) & (at < low + cs)
    base = jnp.sum(jnp.where(inside, low, 0).astype(F32), axis=1, keepdims=True).astype(jnp.int32)
    small_lane = iota((total, LANES), 1) == iota((total, LANES), 0) - base
    marks = jnp.dot(inside.astype(BF16), ids_recv[:, 0, 0:LANES].astype(BF16), preferred_element_type=F32)
    marks = jnp.where(small_lane, marks, 0.0)
    small_col = jnp.sum(marks, axis=1, keepdims=True)
    small_row = nt(jnp.ones((8, LANES), BF16), marks.astype(BF16))[0:1]

    big_total = n * cb
    low = iota((big_total, n), 1) * cb
    at = iota((big_total, n), 0)
    inside = (at >= low) & (at < low + cb)
    base = jnp.sum(jnp.where(inside, low, 0).astype(F32), axis=1, keepdims=True).astype(jnp.int32)
    marks = jnp.dot(inside.astype(BF16), ids_recv[:, 0, LANES:].astype(BF16), preferred_element_type=F32)
    big_marks[...] = jnp.where(iota((big_total, LANES), 1) == iota((big_total, LANES), 0) - base, marks, 0.0)

    my_row = nt(jnp.ones((8, LANES), BF16), big_marks[0:group, :].astype(BF16))[0:1]
    best = jnp.full((1, group), -1.0, F32)
    for r in range(shards):
        if r:
            two_copy(r).wait_recv()
            if r % cores == 0 and cores > 1:
                two_copy(r + 1).start()
        theirs = pl.ds(r * group, group)
        scores = nt(big_all[theirs, :], big_all[0:group, :])
        allowed = jnp.sum(big_marks[theirs, :], axis=1, keepdims=True) == my_row
        if r == 0:
            allowed = allowed & (iota((group, group), 0) != iota((group, group), 1))
        best = jnp.maximum(best, jnp.max(jnp.where(allowed, scores, -1.0), axis=0, keepdims=True))
    low = iota((up(blocks, 16), group), 0) * cb
    at = iota((up(blocks, 16), group), 1)
    spread = jnp.where((at >= low) & (at < low + cb), best, 0.0)
    place = lax.rem(iota((group, LANES), 0), cb) == iota((group, LANES), 1)
    back = exact_dot(spread, place.astype(F32))
    for b in range(blocks):
        back_send[n + b] = back[b : b + 1]
    for j in far:
        bback_copy(j).start()
    back_recv[n] = back_send[n]

    def small_best(r0, r1, c0, c1):
        scores = nt(small_recv[r0:r1, :], small_recv[c0:c1, :])
        allowed = small_col[r0:r1] == small_row[:, c0:c1]
        if r0 < c1 and c0 < r1:
            allowed = allowed & (iota((r1 - r0, c1 - c0), 0) + r0 != iota((r1 - r0, c1 - c0), 1) + c0)
        return jnp.max(jnp.where(allowed, scores, -1.0), axis=0, keepdims=True)

    width = next(w for w in (256, 128, total) if total % w == 0)
    cut = total - span
    parts = []
    for r in range(shards):
        if r == shards - 1:
            parts = [small_best(0, cut, c, c + width) for c in range(0, cut - width + 1, width)]
        for j in range(blocks):
            if (r, j) != (0, 0):
                (line_copy if j else side_copy)(r, j).wait_recv()
    for c in range(0, total, width):
        late = small_best(cut, total, c, c + width)
        if c // width < len(parts):
            parts[c // width] = jnp.maximum(parts[c // width], late)
        else:
            parts.append(jnp.maximum(small_best(0, cut, c, c + width), late))
    best = jnp.concatenate(parts, axis=1) if len(parts) > 1 else parts[0]
    low = iota((n, total), 0) * cs
    at = iota((n, total), 1)
    spread = jnp.where((at >= low) & (at < low + cs), best, 0.0)
    back = exact_dot(spread, small_lane.astype(F32))
    for q in range(n):
        back_send[q] = back[q : q + 1]
    for q, r, j in peers:
        sback_copy(q, r, j).start()
    back_recv[0] = back_send[0]

    for j in far:
        bback_copy(j).wait_recv()
    for q, r, j in peers:
        sback_copy(q, r, j).wait_recv()
    result = exact_dot(back_recv[:, 0, :], at_rank.astype(F32))
    out_ref[...] = jnp.sum(jnp.where(onehot, result, 0.0), axis=0, keepdims=True)

    for j in far:
        one_copy(j).wait_send()
        bback_copy(j).wait_send()
    for r in range(1, shards):
        two_copy(r).wait_send()
    for q, r, j in peers:
        ids_copy(q, r, j).wait_send()
        sback_copy(q, r, j).wait_send()
        if r:
            side_copy(r, j).wait_send()
        if j:
            line_copy(r, j).wait_send()


def solution(mesh):
    shards, blocks = mesh.shape["docs"], mesh.shape["blk"]
    n = shards * blocks

    def body(pooled, proj_weight, cluster):
        rows, width = pooled.shape
        feature = proj_weight.shape[1]
        big_count = rows // 4
        cap_big = 2 * big_count // shards
        cap_small = 2 * (rows - big_count) // n
        cs = up(cap_small, 16)
        cb = up(cap_big * (shards // blocks), 16)
        nb = up(n + blocks, 16)
        dma = pltpu.SemaphoreType.DMA
        out = pl.pallas_call(
            functools.partial(kernel, (shards, blocks, cs, cb)),
            out_shape=jax.ShapeDtypeStruct((1, rows), F32),
            in_specs=[
                pl.BlockSpec(memory_space=pl.ANY),
                pl.BlockSpec(memory_space=pl.ANY),
                pl.BlockSpec(memory_space=pltpu.VMEM),
            ],
            out_specs=pl.BlockSpec(memory_space=pltpu.VMEM),
            scratch_shapes=[
                pltpu.VMEM((rows, width), BF16),
                pltpu.VMEM((width, feature), BF16),
                pltpu.VMEM((rows, feature), BF16),
                pltpu.VMEM((n * cs, feature), BF16),
                pltpu.VMEM((n * cs, feature), BF16),
                pltpu.VMEM((n * cs, feature), BF16),
                pltpu.VMEM((blocks * cb, feature), BF16),
                pltpu.VMEM((n * cb, feature), BF16),
                pltpu.VMEM((n, 1, 2 * LANES), F32),
                pltpu.VMEM((n, 1, 2 * LANES), F32),
                pltpu.VMEM((n * cb, LANES), F32),
                pltpu.VMEM((n + blocks, 1, LANES), F32),
                pltpu.VMEM((nb, 1, LANES), F32),
                dma((2,)), dma((n,)), dma((n,)), dma((n,)), dma((n,)), dma((n,)), dma((n,)), dma((blocks,)), dma((blocks,)),
                dma((shards,)), dma((shards,)), dma((n,)), dma((n,)), dma((blocks,)), dma((blocks,)),
            ],
            compiler_params=pltpu.CompilerParams(
                collective_id=0, has_side_effects=True, vmem_limit_bytes=60 * 1024 * 1024
            ),
        )(pooled, proj_weight, cluster.reshape(1, rows))
        return jnp.maximum(out.reshape(rows), -1.0)

    in_specs = (P(("slab", "docs", "blk"), None), P(), P(("slab", "docs", "blk")))
    out_specs = P(("slab", "docs", "blk"))
    return jax.shard_map(body, mesh=mesh, in_specs=in_specs, out_specs=out_specs, check_vma=False)
```
